32 devices in a mesh: dp: 8 (over y, x, core), tensor: 4 (over z).
Axes of the slice: x: 2, y: 2, z: 4, core: 2. Of those that a mesh axis runs over, the one named last changes fastest.
Arguments:
- layer_in: bfloat16 [8192, 2048], P(('dp', 'tensor')), may hold values from -6 to 6
- cotangent: bfloat16 [8192, 2048], P(('dp', 'tensor')), may hold values from -6 to 6
- doc_ids: int32 [8192], P('dp'), may hold values from 0 to 3, as said below
- positions: int32 [8192], P('dp'), may hold values from 0 to 511, as said below
- attn_gain: float32 [2048], replicated, may hold values from 0.5 to 1.5
- w_query: bfloat16 [2048, 2048], P(None, 'tensor'), may hold values from -0.125 to 0.125
- w_key: bfloat16 [2048, 2048], P(None, 'tensor'), may hold values from -0.125 to 0.125
- w_value: bfloat16 [2048, 2048], P(None, 'tensor'), may hold values from -0.125 to 0.125
- w_out: bfloat16 [2048, 2048], P('tensor'), may hold values from -3 to 3
- ffn_gain: float32 [2048], replicated, may hold values from 0.5 to 1.5
- w_gate: bfloat16 [2048, 8192], P(None, 'tensor'), may hold values from -0.125 to 0.125
- w_up: bfloat16 [2048, 8192], P(None, 'tensor'), may hold values from -0.125 to 0.125
- w_down: bfloat16 [8192, 2048], P('tensor'), may hold values from -0.0625 to 0.0625
Outputs:
- layer_out: bfloat16 [8192, 2048], P(('dp', 'tensor'))
- in_grad: bfloat16 [8192, 2048], P(('dp', 'tensor'))
- attn_gain_grad: float32 [2048], replicated
- query_grad: float32 [2048, 2048], P(None, 'tensor')
- key_grad: float32 [2048, 2048], P(None, 'tensor')
- value_grad: float32 [2048, 2048], P(None, 'tensor')
- out_grad: float32 [2048, 2048], P('tensor')
- ffn_gain_grad: float32 [2048], replicated
- gate_grad: float32 [2048, 8192], P(None, 'tensor')
- up_grad: float32 [2048, 8192], P(None, 'tensor')
- down_grad: float32 [8192, 2048], P('tensor')
The draws below stay inside these ranges and needn't reach their ends.
Inputs may be any that keep to these rules, and one draw needn't show every extreme that they name: `doc_ids`: within each sequence of 1024 tokens the ids never fall, start at 0 and end at 3: 4 contiguous documents of ragged lengths, one of which holds exactly 512 tokens. `positions`: each token's offset from the first token of its document.
All inputs are finite; a program needn't handle non-finite values.
Results may differ from the reference program's by a relative error of at most 0.018.
Values may be sent and summed in bfloat16 or wider, within the bound.
No kernel may reach another device: no remote copies, remote signals or barrier semaphores. Data moves between devices by JAX's collectives and lax.ppermute only.
A program may use at most 320 MiB of HBM per device.

```python
import math
import jax
import jax.numpy as jnp
from jax import lax

D = 2048
HEADS = 16
HD = 128
FF = 8192
SEQ = 1024
DOCS = 4
TOKENS = 8192


def doc_layout(key):
    seq_count = TOKENS // SEQ
    seq_keys = jax.random.split(jax.random.fold_in(key, 7), seq_count)
    half = SEQ // 2

    def layout_one(one_key):
        cut_key, long_key = jax.random.split(one_key)
        shuffled = jax.random.permutation(cut_key, half - 1).astype(jnp.int32)
        cuts = jnp.sort(shuffled[:DOCS - 2] + 1).astype(jnp.int32)
        small_starts = jnp.concatenate([jnp.zeros((1,), jnp.int32), cuts])
        long_index = jax.random.randint(long_key, (), 0, DOCS).astype(jnp.int32)
        rank = jnp.arange(DOCS - 1, dtype=jnp.int32)
        moved = small_starts + jnp.where(rank >= long_index, half, 0).astype(jnp.int32)
        padded = jnp.concatenate([small_starts, jnp.full((1,), half, jnp.int32)])
        long_start = jnp.sum(jnp.where(jnp.arange(DOCS, dtype=jnp.int32) == long_index, padded, 0)).astype(jnp.int32)
        starts = jnp.concatenate([moved, long_start[None]])
        places = jnp.arange(SEQ, dtype=jnp.int32)
        begun = starts[None, :] <= places[:, None]
        numbers = (jnp.sum(begun.astype(jnp.int32), axis=1) - 1).astype(jnp.int32)
        latest = jnp.max(jnp.where(begun, starts[None, :], 0), axis=1).astype(jnp.int32)
        return (numbers, (places - latest).astype(jnp.int32))
    numbers, offsets = jax.vmap(layout_one)(seq_keys)
    return (numbers.reshape(-1), offsets.reshape(-1))


def draw_doc_ids(key, part):
    return doc_layout(key)[0]


def draw_positions(key, part):
    return doc_layout(key)[1]


def levels(stream_key, dims, cuts, low, high):
    factor_of, own = 1.0, jax.random.fold_in(stream_key, 6)
    for axis_at, blocks in cuts:
        heights = jnp.exp(jax.random.uniform(jax.random.fold_in(own, axis_at), (blocks,), jnp.float32, low / len(cuts), high / len(cuts)))
        factor_of = factor_of * jnp.repeat(heights, dims[axis_at] // blocks).reshape([-1 if axis == axis_at else 1 for axis in range(len(dims))])
    return factor_of


def bell_draw(own_key, shape, deviation, most, cuts=(), held_as=jnp.bfloat16):
    values = jax.random.normal(own_key, shape, jnp.float32) * deviation
    if len(cuts) > 0:
        values = levels(own_key, shape, cuts, -0.22, 0.18) * values
    return jnp.clip(values, min=-most, max=most).astype(held_as)


def setup_inputs(seed: int = 0) -> dict:
    splits = jax.random.split(jax.random.key(seed), 14)
    return {
        "layer_in": bell_draw(splits[0], (TOKENS, D), 1.0, 6.0, ((0, 32),)),
        "cotangent": bell_draw(splits[1], (TOKENS, D), 1.0, 6.0, ((0, 32),)),
        "doc_ids": draw_doc_ids(jax.random.fold_in(splits[13], 71), 0),
        "positions": draw_positions(jax.random.fold_in(splits[13], 71), 0),
        "attn_gain": jnp.clip(1.0 + 0.1 * jax.random.normal(splits[4], (D,), jnp.float32), 0.5, 1.5),
        "w_query": bell_draw(splits[5], (D, D), D ** -0.5, 0.125, ((1, 4),)),
        "w_key": bell_draw(splits[6], (D, D), D ** -0.5, 0.125, ((1, 4),)),
        "w_value": bell_draw(splits[7], (D, D), D ** -0.5, 0.125, ((1, 4),)),
        "w_out": bell_draw(splits[8], (D, D), 4 ** -0.5, 3.0, ((0, 4),)),
        "ffn_gain": jnp.clip(1.0 + 0.1 * jax.random.normal(splits[9], (D,), jnp.float32), 0.5, 1.5),
        "w_gate": bell_draw(splits[10], (D, FF), D ** -0.5, 0.125, ((1, 4),)),
        "w_up": bell_draw(splits[11], (D, FF), D ** -0.5, 0.125, ((1, 4),)),
        "w_down": bell_draw(splits[12], (FF, D), FF ** -0.5, 0.0625, ((0, 4),)),
    }


EPS = 1e-05
ROPE_BASE = 500000.0
HIGH = lax.Precision.HIGHEST

@jax.custom_vjp
def low(v):
    return lax.optimization_barrier(v.astype(jnp.bfloat16)).astype(jnp.float32)

@jax.custom_vjp
def low_back(v):
    return v

def low_keep(v):
    return (low(v), None)

def low_pass(kept, grad):
    return (grad,)

def back_keep(v):
    return (v, None)

def back_low(kept, grad):
    return (low(grad),)
low.defvjp(low_keep, low_pass)
low_back.defvjp(back_keep, back_low)

def rms_scale(values, gain):
    return values * lax.rsqrt(lax.optimization_barrier(jnp.mean(values * values, axis=-1, keepdims=True)) + EPS) * gain

def rope_turn(values, positions):
    half = HD // 2
    freqs = ROPE_BASE ** (-(jnp.arange(half).astype(jnp.float32) * 2.0) / HD)
    angles = positions.astype(jnp.float32)[:, None] * freqs[None, :]
    cosine = jnp.cos(angles)[:, None, :]
    sine = jnp.sin(angles)[:, None, :]
    heads = values.reshape(values.shape[0], -1, HD)
    lower = heads[..., :half]
    upper = heads[..., half:]
    turned = jnp.concatenate([lower * cosine - upper * sine, upper * cosine + lower * sine], axis=-1)
    return turned.reshape(values.shape)

def attend_one(pieces):
    query_s, key_s, value_s, ids_s = pieces
    heads_q = query_s.reshape(SEQ, HEADS, HD)
    heads_k = key_s.reshape(SEQ, HEADS, HD)
    heads_v = value_s.reshape(SEQ, HEADS, HD)
    scores = jnp.einsum('qhd,khd->hqk', heads_q, heads_k, precision=HIGH) / math.sqrt(HD) - math.log(SEQ)
    scores = low_back(scores)
    places = jnp.arange(SEQ)
    allowed = (ids_s[:, None] == ids_s[None, :]) & (places[:, None] >= places[None, :])
    probs = low(jnp.where(allowed[None], jax.nn.sigmoid(scores), 0.0))
    mixed = jnp.einsum('hqk,khd->qhd', probs, heads_v, precision=HIGH).reshape(SEQ, HEADS * HD)
    return low(low_back(mixed))

def forward(layer_f, doc_ids, positions, attn_gain, w_query, w_key, w_value, w_out, ffn_gain, w_gate, w_up, w_down):
    normed = low(rms_scale(layer_f, attn_gain))
    query_pre = low_back(jnp.dot(normed, w_query, precision=HIGH))
    key_pre = low_back(jnp.dot(normed, w_key, precision=HIGH))
    value = low(low_back(jnp.dot(normed, w_value, precision=HIGH)))
    query = low(rope_turn(query_pre, positions))
    key_rot = low(rope_turn(key_pre, positions))
    seq_count = layer_f.shape[0] // SEQ
    mixed = lax.map(jax.checkpoint(attend_one), (query.reshape(seq_count, SEQ, D), key_rot.reshape(seq_count, SEQ, D), value.reshape(seq_count, SEQ, D), doc_ids.reshape(seq_count, SEQ)))
    mixed = mixed.reshape(seq_count * SEQ, D)
    attn_branch = low_back(jnp.dot(mixed, w_out, precision=HIGH))
    resid = layer_f + attn_branch
    normed2 = low(rms_scale(resid, ffn_gain))
    gate = low_back(jnp.dot(normed2, w_gate, precision=HIGH))
    up_proj = low_back(jnp.dot(normed2, w_up, precision=HIGH))
    inner = low(jax.nn.silu(gate) * up_proj)
    return resid + jnp.dot(inner, w_down, precision=HIGH)

def reference(layer_in, cotangent, doc_ids, positions, attn_gain, w_query, w_key, w_value, w_out, ffn_gain, w_gate, w_up, w_down):
    weights = (attn_gain.astype(jnp.float32), w_query.astype(jnp.float32), w_key.astype(jnp.float32), w_value.astype(jnp.float32), w_out.astype(jnp.float32), ffn_gain.astype(jnp.float32), w_gate.astype(jnp.float32), w_up.astype(jnp.float32), w_down.astype(jnp.float32))
    layer_f = layer_in.astype(jnp.float32)

    def wrapped(layer_v, *params):
        return forward(layer_v, doc_ids, positions, *params)
    result, pullback = jax.vjp(wrapped, layer_f, *weights)
    grads = pullback(cotangent.astype(jnp.float32))
    return (result.astype(jnp.bfloat16), grads[0].astype(jnp.bfloat16), grads[1], grads[2], grads[3], grads[4], grads[5], grads[6], grads[7], grads[8], grads[9])
```

```python
import functools
import math

import jax
import jax.numpy as jnp
from jax import lax
from jax.experimental import pallas as pl
from jax.experimental.pallas import tpu as pltpu
from jax.sharding import PartitionSpec as P

HD = 128
EPS = 1e-05
ROPE_BASE = 500000.0
BF = jnp.bfloat16
F32 = jnp.float32


def mm(left, right):
    return jnp.dot(left, right, preferred_element_type=F32)


def contract_rows(left, right):
    return lax.dot_general(left, right, (((0,), (0,)), ((), ())), preferred_element_type=F32)


def contract_cols(left, right):
    return lax.dot_general(left, right, (((1,), (1,)), ((), ())), preferred_element_type=F32)


def rms_rate(values):
    return lax.rsqrt(jnp.mean(values * values, axis=-1, keepdims=True) + EPS)


def rope_tables(positions):
    half = HD // 2
    freqs = ROPE_BASE ** (-(jnp.arange(half).astype(F32) * 2.0) / HD)
    angles = positions.astype(F32)[:, None] * freqs[None, :]
    return jnp.cos(angles)[:, None, :], jnp.sin(angles)[:, None, :]


def rope_turn(values, cosine, sine):
    half = HD // 2
    heads = values.reshape(values.shape[0], -1, HD)
    lower, upper = heads[..., :half], heads[..., half:]
    turned = jnp.concatenate(
        [lower * cosine - upper * sine, upper * cosine + lower * sine], axis=-1
    )
    return turned.reshape(values.shape)


def rope_back(values, cosine, sine):
    return rope_turn(values, cosine, -sine)


def fence(value):
    return lax.optimization_barrier(value)


class Job:
    def __init__(self, steps):
        self.steps, self.got, self.out, self.live = steps, None, None, True

    def step(self):
        try:
            return self.steps.send(self.got)
        except StopIteration as stop:
            self.out, self.live = stop.value, False
            return None


class Clock:
    def __init__(self, size):
        self.size = size
        self.jobs = []

    def add(self, steps):
        job = Job(steps)
        self.jobs.append(job)
        return job

    def tick(self, values):
        going, waits = [], []
        for job in self.jobs:
            wait = job.step()
            if job.live:
                going.append(job)
                waits.append(wait)
        values, waits = fence((values, waits))
        for job, wait in zip(going, waits):
            job.got = wait
        self.jobs = going
        return values

    def hop(self, *values):
        ring = [(i, (i + 1) % self.size) for i in range(self.size)]
        moved = self.tick([lax.ppermute(v, "tensor", ring) for v in values])
        return moved[0] if len(moved) == 1 else moved

    def drain(self):
        while self.jobs:
            self.tick([])


def join_kernel(widths, halves, bit_ref, mine_ref, other_ref, *out_refs):
    own = pl.program_id(0) // halves == bit_ref[0]

    def write(source):
        at = 0
        for width, out in zip(widths, out_refs):
            out[...] = source[:, at : at + width].astype(F32)
            at += width

    @pl.when(own)
    def _():
        write(mine_ref)

    @pl.when(jnp.logical_not(own))
    def _():
        write(other_ref)


def join_halves(mine, other, bit, widths):
    rows, width = mine.shape
    block = min(256, rows)
    halves = rows // block
    last = halves - 1

    def place(start):
        return lambda i, bits: (jnp.clip(i - start(bits[0]) * halves, 0, last), 0)

    return pl.pallas_call(
        functools.partial(join_kernel, widths, halves),
        out_shape=[jax.ShapeDtypeStruct((2 * rows, w), F32) for w in widths],
        grid_spec=pltpu.PrefetchScalarGridSpec(
            num_scalar_prefetch=1,
            grid=(2 * halves,),
            in_specs=[
                pl.BlockSpec((block, width), place(lambda b: b)),
                pl.BlockSpec((block, width), place(lambda b: 1 - b)),
            ],
            out_specs=[pl.BlockSpec((block, w), lambda i, bits: (i, 0)) for w in widths],
        ),
        cost_estimate=pl.CostEstimate(
            flops=2 * rows * width, bytes_accessed=12 * rows * width, transcendentals=0
        ),
    )(bit.reshape(1), mine, other)


def ffn_kernel(normed_ref, cot_ref, gate_ref, up_ref, down_ref, inner_ref, d_gate_ref, d_up_ref,
               pull_ref, out_ref, sum_ref):
    step = pl.program_id(0)

    @pl.when(step == 0)
    def _():
        pull_ref[...] = jnp.zeros_like(pull_ref)
        sum_ref[...] = jnp.zeros_like(sum_ref)

    gate = mm(normed_ref[...], gate_ref[...])
    up = mm(normed_ref[...], up_ref[...])
    d_inner = contract_cols(cot_ref[...], down_ref[...])
    sig = jax.nn.sigmoid(gate)
    silu = gate * sig
    inner = (silu * up).astype(BF)
    d_gate = (d_inner * up * (sig * (1.0 + gate * (1.0 - sig)))).astype(BF)
    d_up = (d_inner * silu).astype(BF)
    inner_ref[...] = inner
    d_gate_ref[...] = d_gate
    d_up_ref[...] = d_up
    pull_ref[...] += contract_cols(d_gate, gate_ref[...]) + contract_cols(d_up, up_ref[...])
    sum_ref[...] += mm(inner, down_ref[...])

    @pl.when(step == pl.num_programs(0) - 1)
    def _():
        out_ref[...] = sum_ref[...].astype(BF)


def ffn_slot(normed2, cot, w_gate, w_up, w_down):
    rows, width = normed2.shape
    hidden = w_gate.shape[1]
    block = min(512, hidden)
    whole = pl.BlockSpec((rows, width), lambda f: (0, 0))
    strip = pl.BlockSpec((rows, block), lambda f: (0, f))
    by_col = pl.BlockSpec((width, block), lambda f: (0, f))
    hidden_out = jax.ShapeDtypeStruct((rows, hidden), BF)
    return pl.pallas_call(
        ffn_kernel,
        out_shape=[
            hidden_out,
            hidden_out,
            hidden_out,
            jax.ShapeDtypeStruct((rows, width), F32),
            jax.ShapeDtypeStruct((rows, width), BF),
        ],
        grid=(hidden // block,),
        in_specs=[whole, whole, by_col, by_col, pl.BlockSpec((block, width), lambda f: (f, 0))],
        out_specs=[strip, strip, strip, whole, whole],
        scratch_shapes=[pltpu.VMEM((rows, width), F32)],
        cost_estimate=pl.CostEstimate(
            flops=12 * rows * width * hidden,
            bytes_accessed=6 * width * hidden + 6 * rows * hidden + 10 * rows * width,
            transcendentals=rows * hidden,
        ),
    )(normed2, cot, w_gate, w_up, w_down)


class Tree:
    def __init__(self, size):
        self.size = size
        self.depth = size.bit_length() - 1
        self.even = size == 1 << self.depth and self.depth > 0
        place = lax.axis_index("dp")
        self.bits = [lax.rem(lax.div(place, jnp.int32(1 << k)), jnp.int32(2)) for k in range(self.depth)]

    def swap(self, value, k):
        return lax.ppermute(value, "dp", [(i, i ^ (1 << k)) for i in range(self.size)])

    def half(self, value, bit, axis=0):
        count = value.shape[axis] // 2
        return lax.dynamic_slice_in_dim(value, bit * count, count, axis)

    def order(self, mine, other, bit):
        return jnp.where(bit == 1, other, mine), jnp.where(bit == 1, mine, other)

    def weight_grad(self, left, right, widths=None):
        widths = widths or (right.shape[1],)
        if not self.even:
            whole = lax.psum(contract_rows(left, right).astype(BF), "dp").astype(F32)
            (whole,) = yield [whole]
            out, at = [], 0
            for width in widths:
                out.append(whole[:, at : at + width])
                at += width
            return out
        core = self.bits[0]
        sent = self.swap(contract_rows(self.half(left, 1 - core, 1), right).astype(BF), 0)
        kept = (contract_rows(self.half(left, core, 1), right) + sent.astype(F32)).astype(BF)
        (kept,) = yield [kept]
        rest = list(range(1, self.depth))
        count = kept.shape[0] // 2
        orders = [rest, rest[::-1]]
        pieces = [kept[:count], kept[count:]]
        for step in range(len(rest)):
            ks = [order[step] for order in orders]
            got = yield [self.swap(self.half(p, 1 - self.bits[k]), k) for p, k in zip(pieces, ks)]
            pieces = [self.half(p, self.bits[k]) + g for p, k, g in zip(pieces, ks, got)]
        lists = [[p] for p in pieces]
        for step in reversed(range(len(rest))):
            ks = [order[step] for order in orders]
            got = yield [[self.swap(p, k) for p in ps] for ps, k in zip(lists, ks)]
            for n, k in enumerate(ks):
                pairs = [self.order(p, o, self.bits[k]) for p, o in zip(lists[n], got[n])]
                lists[n] = [p[0] for p in pairs] + [p[1] for p in pairs]
        mine = jnp.concatenate(lists[0] + lists[1], axis=0)
        out = join_halves(mine, self.swap(mine, 0), core, widths)
        out = yield out
        return out

    def sum_small(self, value, tensor_size):
        if not self.even or tensor_size & (tensor_size - 1):
            return lax.psum(value, ("dp", "tensor"))
        k = 1
        while k < tensor_size:
            value = value + lax.ppermute(value, "tensor", [(i, i ^ k) for i in range(tensor_size)])
            k *= 2
        for k in range(self.depth):
            value = value + self.swap(value, k)
        return value


def local(dp_size, tensor_size, layer_in, cotangent, doc_ids, positions, attn_gain, w_query, w_key,
          w_value, w_out, ffn_gain, w_gate, w_up, w_down):
    clock = Clock(tensor_size)
    tree = Tree(dp_size)
    me = lax.axis_index("tensor")
    seq_len = doc_ids.shape[0]
    rows, width = layer_in.shape
    local_width = w_query.shape[1]
    heads = local_width // HD
    scale = 1.0 / math.sqrt(HD)
    slots = range(tensor_size)
    outward = list(range(1, tensor_size)) + [0]
    last = tensor_size - 1

    def owner(k):
        return lax.rem(me + tensor_size - k, tensor_size)

    def slot_rows(vector, k):
        return lax.dynamic_slice_in_dim(vector, owner(k) * rows, rows, 0)

    def join(parts):
        return jnp.concatenate(parts, axis=0)

    places = [owner(k) * rows + jnp.arange(rows) for k in slots]
    docs = [slot_rows(doc_ids, k) for k in slots]
    tables = [rope_tables(slot_rows(positions, k)) for k in slots]
    all_places, all_docs = join(places), join(docs)
    cosine, sine = join([t[0] for t in tables]), join([t[1] for t in tables])

    own_in = layer_in.astype(F32)
    rate1 = rms_rate(own_in)
    normed = [(own_in * rate1 * attn_gain).astype(BF)]
    for _ in range(last):
        normed.append(clock.hop(normed[-1]))
    cots = [cotangent]
    if last:
        cots.append(clock.hop(cotangent))
    query_slots, key_slots, value_slots = [], [], []
    for k in slots:
        query_slots.append(rope_turn(mm(normed[k], w_query), *tables[k]).astype(BF))
        key_slots.append(rope_turn(mm(normed[k], w_key), *tables[k]).astype(BF))
        value_slots.append(mm(normed[k], w_value).astype(BF))
    key_heads = join(key_slots).reshape(seq_len, heads, HD)
    value_heads = join(value_slots).reshape(seq_len, heads, HD)

    def block(k):
        query_blk = query_slots[k].reshape(rows, heads, HD)
        scores = jnp.einsum("qhd,khd->hqk", query_blk, key_heads, preferred_element_type=F32)
        scores = scores * scale - math.log(seq_len)
        allowed = (docs[k][:, None] == all_docs[None, :]) & (
            places[k][:, None] >= all_places[None, :]
        )
        return query_blk, jax.nn.sigmoid(scores), allowed[None]

    mixed_slots, attn_parts = [None] * tensor_size, [None] * tensor_size
    for k in outward:
        _, sigmas, allowed = block(k)
        probs = jnp.where(allowed, sigmas, 0.0).astype(BF)
        mixed = jnp.einsum("hqk,khd->qhd", probs, value_heads, preferred_element_type=F32)
        mixed_slots[k] = mixed.reshape(rows, local_width).astype(BF)
        attn_parts[k] = fence(mm(mixed_slots[k], w_out))
    total = attn_parts[0]
    if last:
        moving = attn_parts[1].astype(BF)
        for k in range(1, tensor_size):
            if len(cots) < tensor_size:
                moving, cot = clock.hop(moving, cots[-1])
                cots.append(cot)
            else:
                moving = clock.hop(moving)
            if k < last:
                moving = (attn_parts[k + 1] + moving.astype(F32)).astype(BF)
        total = total + moving.astype(F32)
    resid = own_in + total
    rate2 = rms_rate(resid)

    normed2, ffn, moving, sent = [(resid * rate2 * ffn_gain).astype(BF)], [], None, 0

    def outgoing(k, moving):
        mine = ffn[k][3]
        return (mine if moving is None else mine + moving.astype(F32)).astype(BF)

    for k in range(1, tensor_size):
        values = [normed2[-1]]
        if k >= 3:
            values.append(outgoing(k - 2, moving))
            sent = k - 2
        moved = clock.hop(*values)
        if k >= 3:
            moved, moving = moved
        ffn.append(ffn_slot(normed2[k - 1], cots[k - 1], w_gate, w_up, w_down))
        normed2.append(moved)
    ffn.append(ffn_slot(normed2[last], cots[last], w_gate, w_up, w_down))
    for k in range(sent + 1, tensor_size):
        if k == last:
            down_job = clock.add(tree.weight_grad(join([f[0] for f in ffn]), join(cots)))
        moving = clock.hop(outgoing(k, moving))
    d_normed2 = ffn[0][3]
    if last:
        d_normed2 = d_normed2 + moving.astype(F32)
    else:
        down_job = clock.add(tree.weight_grad(ffn[0][0], cotangent))

    unit2 = resid * rate2
    ffn_gain_part = jnp.sum(d_normed2 * unit2, axis=0)
    pulled = d_normed2 * ffn_gain
    d_resid = cotangent.astype(F32) + rate2 * (
        pulled - unit2 * jnp.mean(pulled * unit2, axis=-1, keepdims=True)
    )
    all_normed2 = join(normed2)
    resid_slots = [d_resid.astype(BF)]
    for k in range(1, tensor_size):
        if k == 2:
            gate_job = clock.add(tree.weight_grad(all_normed2, join([f[1] for f in ffn])))
        resid_slots.append(clock.hop(resid_slots[-1]))
    if last < 2:
        gate_job = clock.add(tree.weight_grad(all_normed2, join([f[1] for f in ffn])))

    d_key = jnp.zeros((seq_len, heads, HD), F32)
    d_value = jnp.zeros((seq_len, heads, HD), F32)
    d_query_slots = []
    for k in slots:
        query_blk, sigmas, allowed = block(k)
        probs = jnp.where(allowed, sigmas, 0.0).astype(BF)
        d_mix = contract_cols(resid_slots[k], w_out).astype(BF).reshape(rows, heads, HD)
        d_probs = jnp.einsum("qhd,khd->hqk", d_mix, value_heads, preferred_element_type=F32)
        d_scores = jnp.where(allowed, d_probs * sigmas * (1.0 - sigmas), 0.0).astype(BF)
        d_value = d_value + jnp.einsum("hqk,qhd->khd", probs, d_mix, preferred_element_type=F32)
        d_query = jnp.einsum("hqk,khd->qhd", d_scores, key_heads, preferred_element_type=F32)
        d_query_slots.append(rope_back((d_query * scale).reshape(rows, local_width), *tables[k]).astype(BF))
        d_key = d_key + jnp.einsum("hqk,qhd->khd", d_scores, query_blk, preferred_element_type=F32)

    up_job = clock.add(tree.weight_grad(all_normed2, join([f[2] for f in ffn])))
    out_job = clock.add(tree.weight_grad(join(mixed_slots), join(resid_slots)))
    total = ffn[0][4].astype(F32)
    if last:
        moving = ffn[1][4]
        for k in range(1, tensor_size):
            moving = clock.hop(moving)
            if k < last:
                moving = (ffn[k + 1][4].astype(F32) + moving.astype(F32)).astype(BF)
        total = total + moving.astype(F32)
    layer_out = (resid + total).astype(BF)

    d_query_pre = join(d_query_slots)
    d_key_pre = rope_back((d_key * scale).reshape(seq_len, local_width), cosine, sine).astype(BF)
    d_value_b = d_value.reshape(seq_len, local_width).astype(BF)
    d_qkv = jnp.concatenate([d_query_pre, d_key_pre, d_value_b], axis=1)
    qkv_job = clock.add(tree.weight_grad(join(normed), d_qkv, (local_width,) * 3))

    def part(array, k):
        return array[k * rows : (k + 1) * rows]

    pulls = [
        fence(
            contract_cols(part(d_query_pre, k), w_query)
            + contract_cols(part(d_key_pre, k), w_key)
            + contract_cols(part(d_value_b, k), w_value)
        )
        for k in slots
    ]
    d_normed = pulls[0]
    if last:
        moving = pulls[1].astype(BF)
        for k in range(1, tensor_size):
            moving = clock.hop(moving)
            if k < last:
                moving = (pulls[k + 1] + moving.astype(F32)).astype(BF)
        d_normed = d_normed + moving.astype(F32)
    unit1 = own_in * rate1
    attn_gain_part = jnp.sum(d_normed * unit1, axis=0)
    pulled1 = d_normed * attn_gain
    in_grad = (
        d_resid + rate1 * (pulled1 - unit1 * jnp.mean(pulled1 * unit1, axis=-1, keepdims=True))
    ).astype(BF)
    gains = tree.sum_small(jnp.stack([attn_gain_part, ffn_gain_part]), tensor_size)
    clock.drain()
    (down_grad,), (gate_grad,), (up_grad,), (out_grad,) = down_job.out, gate_job.out, up_job.out, out_job.out
    query_grad, key_grad, value_grad = qkv_job.out
    return (layer_out, in_grad, gains[0], query_grad, key_grad, value_grad, out_grad, gains[1],
            gate_grad, up_grad, down_grad)


def solution(mesh):
    by_row = P(("dp", "tensor"), None)
    by_col = P(None, "tensor")
    by_top = P("tensor", None)
    dp_size, tensor_size = mesh.shape["dp"], mesh.shape["tensor"]

    def body(*arrays):
        return local(dp_size, tensor_size, *arrays)

    return jax.shard_map(
        body,
        mesh=mesh,
        in_specs=(by_row, by_row, P("dp"), P("dp"), P(), by_col, by_col, by_col, by_top, P(), by_col,
                  by_col, by_top),
        out_specs=(by_row, by_row, P(), by_col, by_col, by_col, by_top, P(), by_col, by_col, by_top),
        check_vma=False,
    )
```
